32 devices in a mesh: section: 8 (over y, x, core), expert: 4 (over z).
Axes of the slice: x: 2, y: 2, z: 4, core: 2. Of those that a mesh axis runs over, the one named last changes fastest.
Arguments:
- acts: bfloat16 [8, 128, 2560], P('section', 'expert'), may hold values from -6 to 6
- incoming: bfloat16 [1, 128, 2560], P(None, 'expert'), may hold values from -6 to 6
- routes: int32 [2, 8, 128, 2], P(None, 'section', 'expert'), may hold values from 0 to 3, all different within a row; in each aligned block of 32 rows (0 to 31, 32 to 63, ..., all dimensions but the last counted through in order) at most 24 rows name the same one
- route_weight: float32 [2, 8, 128, 2], P(None, 'section', 'expert'), may hold values from 0.25 to 1
- norm_gain: float32 [8, 2560], P('section'), may hold values from 0.25 to 1.75
- w_gate: bfloat16 [8, 2560, 3072], P('section', None, 'expert'), may hold values from -0.125 to 0.125
- w_up: bfloat16 [8, 2560, 3072], P('section', None, 'expert'), may hold values from -0.125 to 0.125
- w_down: bfloat16 [8, 3072, 2560], P('section', 'expert'), may hold values from -0.21875 to 0.21875
Outputs:
- section_outputs: bfloat16 [2, 8, 128, 2560], P(None, 'section', 'expert')
The draws below stay inside these ranges and needn't reach their ends.
Inputs may be any that keep to these rules, and one draw needn't show every extreme that they name: `routes`: a token's 2 experts are distinct; in each aligned block of 32 tokens (the tokens of one device) no expert is chosen more than 24 times, and that count is reached.
All inputs are finite; a program needn't handle non-finite values.
Results may differ from the reference program's by a relative error of at most 0.009.
Values may be sent and summed in bfloat16 or wider, within the bound.
A program may use at most 64 MiB of HBM per device.

```python
import math
import jax
import jax.numpy as jnp
import numpy as np
from jax import lax

D = 2560
FF = 768
EXPERTS = 4
TOP = 2
TICKS = 2
TOK_DEV = 32
CAP = 24
GROUP = 128
N_SECTION = 8
N_EXPERT = 4


def block_scale(rng, extent, pieces, low, largest):
    factor_of, own = 1.0, jax.random.fold_in(rng, 6)
    for position, shards_of in pieces:
        draws = jnp.exp(jax.random.uniform(jax.random.fold_in(own, position), (shards_of,), jnp.float32, low / len(pieces), largest / len(pieces)))
        factor_of = factor_of * jnp.repeat(draws, extent[position] // shards_of).reshape([-1 if axis == position else 1 for axis in range(len(extent))])
    return factor_of


def routed_block(own_key, own, number, rows, amount, top, most, skew):
    order = jax.random.permutation(own_key, amount)
    packed, common = portions_of(amount, rows * top, most, skew, True), portions_of(amount, rows * top, most, skew, False)
    places = jnp.arange(amount)

    def named(lengths, offset_by):
        used = int((lengths > 0).sum())
        fixed = max(1, used // 4)
        shifted = fixed + (places - fixed + offset_by * (used - fixed)) % max(1, amount - fixed)
        return jnp.zeros((amount,), jnp.int32).at[order[jnp.where(places < fixed, places, shifted)]].set(jnp.asarray(lengths, jnp.int32))

    lengths = jnp.where(number % 4 == 0, named(packed, number // 4), named(common, number - number // 4 - 1))
    mixed = jax.random.permutation(jax.random.fold_in(own, 3), amount)
    giver, receiver = mixed[0:amount // 2 * 2:2], mixed[1:amount // 2 * 2:2]
    margin = jnp.minimum(lengths[giver] - 1, most - lengths[receiver]) // 2
    margin = jnp.where((giver == order[0]) | (receiver == order[0]) | (lengths[receiver] == 0), 0, jnp.maximum(margin, 0))
    shifted = jax.random.randint(jax.random.fold_in(own, 4), (amount // 2,), 0, 1 << 20) % (margin + 1)
    lengths = lengths.at[giver].add(-shifted).at[receiver].add(shifted)
    items = jnp.searchsorted(jnp.cumsum(lengths), jnp.arange(rows * top), side="right").astype(jnp.int32)
    grid = items.reshape(top, rows).T
    grid = grid[jax.random.permutation(jax.random.fold_in(own, 1), rows)]
    offset_by = jax.random.randint(jax.random.fold_in(own, 2), (rows, 1), 0, top)
    return jnp.take_along_axis(grid, (jnp.arange(top)[None, :] + offset_by) % top, axis=1)


def portions_of(number_of, total, most, slope, full):
    portions = [(1 << 20) // math.isqrt(rank ** slope) + 1 for rank in range(1, number_of + 1)]
    largest = most if full else min(most, max(-(-total // number_of), total * portions[0] // sum(portions)))
    least = 1 if total - largest >= number_of - 1 else 0
    given, spare = [largest] + [least] * (number_of - 1), total - largest - least * (number_of - 1)
    while spare > 0:
        candidates = [i for i in range(1, number_of) if given[i] < largest] or [i for i in range(1, number_of) if given[i] < most]
        pool, budget = sum([portions[i] for i in candidates]), spare
        for i in candidates:
            addition = min(most - given[i], max(1, budget * portions[i] // pool), spare)
            given[i] = given[i] + addition
            spare = spare - addition
    return np.array(given)


def noise(own_key, shape, spread, limit, pieces=(), kind=jnp.bfloat16):
    drawn = spread * jax.random.normal(own_key, shape, jnp.float32)
    if pieces:
        drawn = drawn * block_scale(own_key, shape, pieces, -0.22, 0.18)
    return jnp.clip(drawn, -limit, limit).astype(kind)


def setup_inputs(seed: int = 0) -> dict:
    keys = jax.random.split(jax.random.key(seed), 9)
    acts = noise(keys[0], (N_SECTION, GROUP, D), 1.0, 6.0, ((0, 8), (1, 4)))
    incoming = noise(keys[1], (TICKS - 1, GROUP, D), 1.0, 6.0, ((1, 4),))
    routes_keys = jax.random.split(jax.random.fold_in(keys[2], 1), TICKS * N_SECTION * GROUP // TOK_DEV)
    routes_turns = jax.random.permutation(jax.random.fold_in(keys[2], 3), TICKS * N_SECTION * GROUP // TOK_DEV)
    routes = jax.vmap(lambda own, number: routed_block(jax.random.fold_in(keys[2], 2), own, number, TOK_DEV, EXPERTS, TOP, CAP, 2))(routes_keys, routes_turns).reshape((TICKS, N_SECTION, GROUP, TOP))
    route_weight = jnp.clip(0.25 + 0.75 * jax.random.uniform(keys[3], (TICKS, N_SECTION, GROUP, TOP), jnp.float32) ** block_scale(keys[3], (TICKS, N_SECTION, GROUP, TOP), ((1, 8), (2, 4)), -0.2, 0.2), 0.25, 1.0)
    norm_gain = jnp.clip(1.0 + 0.15 * jax.random.normal(keys[4], (N_SECTION, D), jnp.float32), 0.25, 1.75)
    w_gate = noise(keys[5], (N_SECTION, D, EXPERTS * FF), D ** -0.5, 0.125, ((0, 8), (2, 4)))
    w_up = noise(keys[6], (N_SECTION, D, EXPERTS * FF), D ** -0.5, 0.125, ((0, 8), (2, 4)))
    w_down = noise(keys[7], (N_SECTION, EXPERTS * FF, D), FF ** -0.5, 0.21875, ((0, 8), (1, 4)))
    return {"acts": acts, "incoming": incoming, "routes": routes, "route_weight": route_weight, "norm_gain": norm_gain, "w_gate": w_gate, "w_up": w_up, "w_down": w_down}


def section_layer(tokens_in, chosen, chosen_weight, gain, w_gate, w_up, w_down):
    blocks = N_EXPERT
    group = N_EXPERT // EXPERTS
    width = EXPERTS * FF // N_EXPERT
    tok_f = tokens_in.astype(jnp.float32)
    normed = (tok_f * lax.rsqrt(lax.optimization_barrier(jnp.mean(tok_f * tok_f, axis=-1, keepdims=True)) + 1e-06) * gain).astype(jnp.bfloat16)
    gate_val = jnp.dot(normed, w_gate, preferred_element_type=jnp.float32)
    up_val = jnp.dot(normed, w_up, preferred_element_type=jnp.float32)
    hidden = (jax.nn.silu(gate_val) * up_val).astype(jnp.bfloat16)
    hidden_b = hidden.reshape(hidden.shape[0], blocks, width).astype(jnp.float32)
    down_b = w_down.reshape(blocks, width, w_down.shape[1]).astype(jnp.float32)
    partial_value = jnp.einsum('tbh,bhd->btd', hidden_b, down_b, precision=lax.Precision.HIGHEST).astype(jnp.bfloat16)
    summed = partial_value.astype(jnp.float32).reshape(EXPERTS, group, hidden.shape[0], w_down.shape[1]).sum(axis=1)
    expert_hot = (chosen[:, :, None] == jnp.arange(EXPERTS, dtype=jnp.int32)[None, None, :]).astype(jnp.float32)
    mixing = lax.optimization_barrier(jnp.sum(chosen_weight[:, :, None] * expert_hot, axis=1))
    routed = jnp.einsum('te,etd->td', mixing, summed, precision=lax.Precision.HIGHEST)
    return (tok_f + routed).astype(jnp.bfloat16)

def reference(acts, incoming, routes, route_weight, norm_gain, w_gate, w_up, w_down):
    state = acts
    results = []
    for tick in range(TICKS):
        layer_out = lax.map(lambda items: section_layer(*items), (state, routes[tick], route_weight[tick], norm_gain, w_gate, w_up, w_down))
        results.append(layer_out)
        if tick + 1 < TICKS:
            state = jnp.concatenate([incoming[tick][None], layer_out[:-1]], axis=0)
    return jnp.stack(results)
```

```python
import functools

import jax
import jax.numpy as jnp
from jax import lax
from jax.experimental import pallas as pl
from jax.experimental.pallas import tpu as pltpu
from jax.sharding import PartitionSpec as P

MESH = pl.DeviceIdType.MESH
EXPERTS = 4
CHUNKS = 2
RIGHT, LEFT = 0, 1


def kernel(
    n,
    sections,
    acts,
    incoming,
    routes,
    route_weight,
    gain,
    w_gate_hbm,
    w_up_hbm,
    w_down_hbm,
    out,
    w_gate,
    w_up,
    w_down,
    xbuf,
    mixbuf,
    rsin,
    rsout,
    held,
    moved,
    w_sem,
    own_sem,
    inc_sem,
    ag_send,
    ag_recv,
    mix_send,
    mix_recv,
    rs_send,
    rs_recv,
    move_send,
    move_recv,
):
    s = lax.axis_index("section")
    e = lax.axis_index("expert")
    ticks, _, chunks, tokens, cols = xbuf.shape
    group = n // EXPERTS
    width = chunks * cols
    has_right = e < n - 1
    has_left = e > 0
    has_next = s < sections - 1
    has_prev = s > 0
    right = (s, jnp.minimum(e + 1, n - 1))
    left = (s, jnp.maximum(e - 1, 0))
    following = (jnp.minimum(s + 1, sections - 1), e)
    previous = (jnp.maximum(s - 1, 0), e)
    has = (has_right, has_left)
    peer = (right, left)

    weight_copies = [
        pltpu.make_async_copy(src, dst, w_sem.at[i])
        for i, (src, dst) in enumerate(
            ((w_gate_hbm, w_gate), (w_up_hbm, w_up), (w_down_hbm, w_down))
        )
    ]

    def own_copy(c):
        return pltpu.make_async_copy(
            acts.at[:, pl.ds(c * cols, cols)], xbuf.at[0, e, c], own_sem.at[c]
        )

    def inc_copy(t, c):
        return pltpu.make_async_copy(
            incoming.at[t - 1, :, pl.ds(c * cols, cols)], xbuf.at[t, e, c], inc_sem.at[t, c]
        )

    def ag_copy(way, t, j, c):
        return pltpu.make_async_remote_copy(
            xbuf.at[t, j, c],
            xbuf.at[t, j, c],
            ag_send.at[way, t, j, c],
            ag_recv.at[way, t, j, c],
            device_id=peer[way],
            device_id_type=MESH,
        )

    def mix_copy(way, j):
        return pltpu.make_async_remote_copy(
            mixbuf.at[j],
            mixbuf.at[j],
            mix_send.at[way, j],
            mix_recv.at[way, j],
            device_id=peer[way],
            device_id_type=MESH,
        )

    def rs_copy(way, t, j, c):
        return pltpu.make_async_remote_copy(
            rsout.at[t, j, c],
            rsin.at[way, t, j, c],
            rs_send.at[way, t, j, c],
            rs_recv.at[way, t, j, c],
            device_id=peer[way],
            device_id_type=MESH,
        )

    def move_copy(t, c):
        return pltpu.make_async_remote_copy(
            moved.at[t, c],
            xbuf.at[t + 1, e, c],
            move_send.at[t, c],
            move_recv.at[t, c],
            device_id=following,
            device_id_type=MESH,
        )

    for c in range(chunks):
        own_copy(c).start()

    barrier = pltpu.get_barrier_semaphore()
    around = (
        (has_right, right),
        (has_left, left),
        (has_next, following),
        (has_prev, previous),
    )
    for there, device in around:

        @pl.when(there)
        def _():
            pl.semaphore_signal(barrier, inc=1, device_id=device, device_id_type=MESH)

    for copy in weight_copies:
        copy.start()

    @pl.when(jnp.logical_not(has_prev))
    def _():
        for t in range(1, ticks):
            for c in range(chunks):
                inc_copy(t, c).start()

    rows = ticks * tokens
    lanes = mixbuf.shape[2]
    eye = lax.broadcasted_iota(jnp.int32, (rows, lanes), 0) == lax.broadcasted_iota(
        jnp.int32, (rows, lanes), 1
    )
    chosen = routes[...]
    chosen_weight = route_weight[...]
    mixbuf[e] = jnp.zeros_like(mixbuf[e])
    for x in range(EXPERTS):
        column = jnp.sum(jnp.where(chosen == x, chosen_weight, 0.0), axis=1, keepdims=True)
        mixbuf[e, x : x + 1, :] = jnp.sum(
            jnp.where(eye, column, 0.0), axis=0, keepdims=True
        )

    pl.semaphore_wait(barrier, sum(jnp.where(there, 1, 0) for there, _ in around))

    def send_own(t, c):
        for way in (RIGHT, LEFT):

            @pl.when(has[way])
            def _():
                ag_copy(way, t, e, c).start()

    def partial_of(t, j):
        squares = jnp.zeros((tokens, 1), jnp.float32)
        for c in range(chunks):
            piece = xbuf[t, j, c].astype(jnp.float32)
            squares = squares + jnp.sum(piece * piece, axis=1, keepdims=True)
        scale = lax.rsqrt(squares * (1.0 / width) + 1e-06)
        gate_val = up_val = None
        for c in range(chunks):
            span = pl.ds(c * cols, cols)
            normed = (xbuf[t, j, c].astype(jnp.float32) * scale * gain[:, span]).astype(
                jnp.bfloat16
            )
            gate_part = jnp.dot(normed, w_gate[span, :], preferred_element_type=jnp.float32)
            up_part = jnp.dot(normed, w_up[span, :], preferred_element_type=jnp.float32)
            gate_val = gate_part if gate_val is None else gate_val + gate_part
            up_val = up_part if up_val is None else up_val + up_part
        hidden = (jax.nn.silu(gate_val) * up_val).astype(jnp.bfloat16)
        expert = e // group
        row = mixbuf[j, pl.ds(expert, 1), :]
        pick = (
            lax.broadcasted_iota(jnp.int32, (tokens, lanes), 0) + t * tokens
            == lax.broadcasted_iota(jnp.int32, (tokens, lanes), 1)
        )
        mixing = jnp.sum(jnp.where(pick, row, 0.0), axis=1, keepdims=True)
        for c in range(chunks):
            span = pl.ds(c * cols, cols)
            value = jnp.dot(hidden, w_down[:, span], preferred_element_type=jnp.float32) * mixing
            held[j, c] = value
            for way, first in (
                (RIGHT, jnp.logical_and(jnp.logical_not(has_left), j > e)),
                (LEFT, jnp.logical_and(jnp.logical_not(has_right), j < e)),
            ):

                @pl.when(first)
                def _():
                    rsout[t, j, c] = value.astype(jnp.bfloat16)
                    rs_copy(way, t, j, c).start()

    def tick(t, _):
        for c in range(chunks):

            @pl.when(t == 0)
            def _():
                own_copy(c).wait()

            @pl.when(jnp.logical_and(t > 0, has_prev))
            def _():
                move_copy(jnp.maximum(t - 1, 0), c).wait_recv()

            @pl.when(jnp.logical_and(t > 0, jnp.logical_not(has_prev)))
            def _():
                inc_copy(jnp.maximum(t, 1), c).wait()

            send_own(t, c)

        @pl.when(t == 0)
        def _():
            for way in (RIGHT, LEFT):

                @pl.when(has[way])
                def _():
                    mix_copy(way, e).start()

            for copy in weight_copies:
                copy.wait()

        def arrive(k, _):
            for c in range(chunks):
                for way, j in ((RIGHT, e - k), (LEFT, e + k)):

                    @pl.when(jnp.logical_and(k > 0, jnp.logical_and(j >= 0, j < n)))
                    def _():
                        ag_copy(way, t, j, c).wait_recv()

                        @pl.when(has[way])
                        def _():
                            ag_copy(way, t, j, c).start()

                        if c == 0:

                            @pl.when(t == 0)
                            def _():
                                mix_copy(way, j).wait_recv()

                                @pl.when(has[way])
                                def _():
                                    mix_copy(way, j).start()

            def side(way, _):
                j = e + k * (2 * way - 1)

                @pl.when(
                    jnp.logical_and(
                        jnp.logical_and(j >= 0, j < n), jnp.logical_or(k > 0, way == 0)
                    )
                )
                def _():
                    partial_of(t, j)

                return 0

            return lax.fori_loop(0, 2, side, 0)

        lax.fori_loop(0, n, arrive, 0)

        from_right, from_left = 2 * (n - 1 - e), 2 * e
        last = jnp.maximum(from_right, from_left)

        def combine(time, _):
            for c in range(chunks):
                for way, there, k, j in (
                    (LEFT, has_right, time - from_right, e - (time - from_right)),
                    (RIGHT, has_left, time - from_left, e + (time - from_left)),
                ):

                    @pl.when(
                        jnp.logical_and(
                            there, jnp.logical_and(k >= 0, jnp.logical_and(j >= 0, j < n))
                        )
                    )
                    def _():
                        rs_copy(way, t, j, c).wait_recv()
                        total = held[j, c] + rsin[way, t, j, c].astype(jnp.float32)

                        @pl.when(k == 0)
                        def _():
                            held[j, c] = total

                        @pl.when(k > 0)
                        def _():
                            rsout[t, j, c] = total.astype(jnp.bfloat16)
                            rs_copy(way, t, j, c).start()

                @pl.when(time == last)
                def _():
                    layer = (xbuf[t, e, c].astype(jnp.float32) + held[e, c]).astype(jnp.bfloat16)
                    out[t, :, pl.ds(c * cols, cols)] = layer

                    @pl.when(jnp.logical_and(t < ticks - 1, has_next))
                    def _():
                        moved[jnp.minimum(t, ticks - 2), c] = layer
                        move_copy(jnp.minimum(t, ticks - 2), c).start()

            return 0

        lax.fori_loop(0, 3 * (n - 1) + 1, combine, 0)
        return 0

    lax.fori_loop(0, ticks, tick, 0)

    def drain(j, _):
        for way, within in (
            (RIGHT, jnp.logical_and(has_right, j <= e)),
            (LEFT, jnp.logical_and(has_left, j >= e)),
        ):

            @pl.when(within)
            def _():
                mix_copy(way, j).wait_send()
                for t in range(ticks):
                    for c in range(chunks):
                        ag_copy(way, t, j, c).wait_send()

        for way, within in ((RIGHT, j > e), (LEFT, j < e)):

            @pl.when(within)
            def _():
                for t in range(ticks):
                    for c in range(chunks):
                        rs_copy(way, t, j, c).wait_send()

        return 0

    lax.fori_loop(0, n, drain, 0)

    @pl.when(has_next)
    def _():
        for t in range(ticks - 1):
            for c in range(chunks):
                move_copy(t, c).wait_send()


def solution(mesh):
    n = mesh.shape["expert"]
    sections = mesh.shape["section"]

    def shards(acts, incoming, routes, route_weight, norm_gain, w_gate, w_up, w_down):
        ticks, _, tokens, top = routes.shape
        width, hidden = w_gate.shape[1:]
        chunks = CHUNKS
        cols = width // chunks
        lanes = -(-ticks * tokens // 128) * 128
        half = jnp.bfloat16
        anywhere = pl.BlockSpec(memory_space=pl.ANY)
        vmem = pl.BlockSpec(memory_space=pltpu.VMEM)
        dma = pltpu.SemaphoreType.DMA
        result = pl.pallas_call(
            functools.partial(kernel, n, sections),
            out_shape=jax.ShapeDtypeStruct((ticks, tokens, width), half),
            in_specs=[anywhere, anywhere, vmem, vmem, vmem, anywhere, anywhere, anywhere],
            out_specs=vmem,
            scratch_shapes=[
                pltpu.VMEM((width, hidden), half),
                pltpu.VMEM((width, hidden), half),
                pltpu.VMEM((hidden, width), half),
                pltpu.VMEM((ticks, n, chunks, tokens, cols), half),
                pltpu.VMEM((n, 8, lanes), jnp.float32),
                pltpu.VMEM((2, ticks, n, chunks, tokens, cols), half),
                pltpu.VMEM((ticks, n, chunks, tokens, cols), half),
                pltpu.VMEM((n, chunks, tokens, cols), jnp.float32),
                pltpu.VMEM((ticks - 1, chunks, tokens, cols), half),
                dma((3,)),
                dma((chunks,)),
                dma((ticks, chunks)),
                dma((2, ticks, n, chunks)),
                dma((2, ticks, n, chunks)),
                dma((2, n)),
                dma((2, n)),
                dma((2, ticks, n, chunks)),
                dma((2, ticks, n, chunks)),
                dma((ticks - 1, chunks)),
                dma((ticks - 1, chunks)),
            ],
            compiler_params=pltpu.CompilerParams(
                collective_id=0, has_side_effects=True, vmem_limit_bytes=56 << 20
            ),
        )(
            acts[0],
            incoming,
            routes.reshape(ticks * tokens, top),
            route_weight.reshape(ticks * tokens, top),
            norm_gain,
            w_gate[0],
            w_up[0],
            w_down[0],
        )
        return result[:, None]

    return jax.shard_map(
        shards,
        mesh=mesh,
        in_specs=(
            P("section", "expert", None),
            P(None, "expert", None),
            P(None, "section", "expert", None),
            P(None, "section", "expert", None),
            P("section", None),
            P("section", None, "expert"),
            P("section", None, "expert"),
            P("section", "expert", None),
        ),
        out_specs=P(None, "section", "expert", None),
        check_vma=False,
    )
```

```python
import functools

import jax
import jax.numpy as jnp
from jax import lax
from jax.experimental import pallas as pl
from jax.experimental.pallas import tpu as pltpu
from jax.sharding import PartitionSpec as P

MESH = pl.DeviceIdType.MESH
EXPERTS = 4
CHUNKS = 4
PIECES = 1
RIGHT, LEFT = 0, 1


def kernel(
    n,
    sections,
    acts,
    incoming,
    routes,
    route_weight,
    gain,
    w_gate_hbm,
    w_up_hbm,
    w_down_hbm,
    out,
    w_gate,
    w_up,
    w_down,
    xbuf,
    mixbuf,
    rsin,
    rsout,
    held,
    moved,
    w_sem,
    own_sem,
    inc_sem,
    ag_send,
    ag_recv,
    mix_send,
    mix_recv,
    rs_send,
    rs_recv,
    move_send,
    move_recv,
):
    s = lax.axis_index("section")
    e = lax.axis_index("expert")
    ticks, _, chunks, tokens, cols = xbuf.shape
    group = n // EXPERTS
    width = chunks * cols
    has_right = e < n - 1
    has_left = e > 0
    has_next = s < sections - 1
    has_prev = s > 0
    right = (s, jnp.minimum(e + 1, n - 1))
    left = (s, jnp.maximum(e - 1, 0))
    following = (jnp.minimum(s + 1, sections - 1), e)
    previous = (jnp.maximum(s - 1, 0), e)
    has = (has_right, has_left)
    peer = (right, left)

    weight_copies = []
    for i, (src, dst) in enumerate(
        ((w_gate_hbm, w_gate), (w_up_hbm, w_up), (w_down_hbm, w_down))
    ):
        deep = src.shape[0] // PIECES
        weight_copies.append(
            [
                pltpu.make_async_copy(
                    src.at[pl.ds(p * deep, deep)], dst.at[pl.ds(p * deep, deep)], w_sem.at[i, p]
                )
                for p in range(PIECES)
            ]
        )

    def own_copy(c):
        return pltpu.make_async_copy(
            acts.at[:, pl.ds(c * cols, cols)], xbuf.at[0, e, c], own_sem.at[c]
        )

    def inc_copy(t, c):
        return pltpu.make_async_copy(
            incoming.at[t - 1, :, pl.ds(c * cols, cols)], xbuf.at[t, e, c], inc_sem.at[t, c]
        )

    def ag_copy(way, t, j, c):
        return pltpu.make_async_remote_copy(
            xbuf.at[t, j, c],
            xbuf.at[t, j, c],
            ag_send.at[way, t, j, c],
            ag_recv.at[way, t, j, c],
            device_id=peer[way],
            device_id_type=MESH,
        )

    def mix_copy(way, j):
        return pltpu.make_async_remote_copy(
            mixbuf.at[j],
            mixbuf.at[j],
            mix_send.at[way, j],
            mix_recv.at[way, j],
            device_id=peer[way],
            device_id_type=MESH,
        )

    def rs_copy(way, t, j, c):
        return pltpu.make_async_remote_copy(
            rsout.at[t, j, c],
            rsin.at[way, t, j, c],
            rs_send.at[way, t, j, c],
            rs_recv.at[way, t, j, c],
            device_id=peer[way],
            device_id_type=MESH,
        )

    def move_copy(t, c):
        return pltpu.make_async_remote_copy(
            moved.at[t, c],
            xbuf.at[t + 1, e, c],
            move_send.at[t, c],
            move_recv.at[t, c],
            device_id=following,
            device_id_type=MESH,
        )

    for c in range(chunks):
        own_copy(c).start()

    barrier = pltpu.get_barrier_semaphore()
    around = (
        (has_right, right),
        (has_left, left),
        (has_next, following),
        (has_prev, previous),
    )
    for there, device in around:

        @pl.when(there)
        def _():
            pl.semaphore_signal(barrier, inc=1, device_id=device, device_id_type=MESH)

    for copies in weight_copies:
        for copy in copies:
            copy.start()

    @pl.when(jnp.logical_not(has_prev))
    def _():
        for t in range(1, ticks):
            for c in range(chunks):
                inc_copy(t, c).start()

    lanes = mixbuf.shape[2]
    mixbuf[e] = jnp.zeros_like(mixbuf[e])
    for t in range(ticks):
        chosen = routes[t, 0]
        chosen_weight = route_weight[t, 0]
        for x in range(EXPERTS):
            mixbuf[e, t * EXPERTS + x : t * EXPERTS + x + 1, 0:tokens] = jnp.sum(
                jnp.where(chosen == x, chosen_weight, 0.0), axis=0, keepdims=True
            )

    pl.semaphore_wait(barrier, sum(jnp.where(there, 1, 0) for there, _ in around))

    def send_own(t, c):
        for way in (RIGHT, LEFT):

            @pl.when(has[way])
            def _():
                ag_copy(way, t, e, c).start()

    def partial_of(t, blocks, first):
        scales = []
        for j in blocks:
            squares = jnp.zeros((tokens, 1), jnp.float32)
            for c in range(chunks):
                piece = xbuf[t, j, c].astype(jnp.float32)
                squares = squares + jnp.sum(piece * piece, axis=1, keepdims=True)
            scales.append(lax.rsqrt(squares * (1.0 / width) + 1e-06))

        @pl.when(first)
        def _():
            for copy in weight_copies[0] + weight_copies[1]:
                copy.wait()

        gate_val = up_val = None
        for c in range(chunks):
            span = pl.ds(c * cols, cols)
            normed = jnp.concatenate(
                [
                    (xbuf[t, j, c].astype(jnp.float32) * scale * gain[:, span]).astype(jnp.bfloat16)
                    for j, scale in zip(blocks, scales)
                ],
                axis=0,
            )
            gate_part = jnp.dot(normed, w_gate[span, :], preferred_element_type=jnp.float32)
            up_part = jnp.dot(normed, w_up[span, :], preferred_element_type=jnp.float32)
            gate_val = gate_part if gate_val is None else gate_val + gate_part
            up_val = up_part if up_val is None else up_val + up_part
        hidden = (jax.nn.silu(gate_val) * up_val).astype(jnp.bfloat16)
        expert = e // group
        pick = lax.broadcasted_iota(jnp.int32, (tokens, lanes), 0) == lax.broadcasted_iota(
            jnp.int32, (tokens, lanes), 1
        )
        mixing = [
            jnp.sum(
                jnp.where(pick, mixbuf[j, pl.ds(t * EXPERTS + expert, 1), :], 0.0),
                axis=1,
                keepdims=True,
            )
            for j in blocks
        ]

        @pl.when(first)
        def _():
            for copy in weight_copies[2]:
                copy.wait()

        for c in range(chunks):
            span = pl.ds(c * cols, cols)
            values = jnp.dot(hidden, w_down[:, span], preferred_element_type=jnp.float32)
            for i, j in enumerate(blocks):
                value = values[i * tokens : (i + 1) * tokens] * mixing[i]
                held[j, c] = value
                if len(blocks) > 1:
                    continue
                for way, send in (
                    (RIGHT, jnp.logical_and(jnp.logical_not(has_left), j > e)),
                    (LEFT, jnp.logical_and(jnp.logical_not(has_right), j < e)),
                ):

                    @pl.when(send)
                    def _():
                        rsout[t, j, c] = value.astype(jnp.bfloat16)
                        rs_copy(way, t, j, c).start()

    def tick(t, _):
        for c in range(chunks):

            @pl.when(t == 0)
            def _():
                own_copy(c).wait()

            @pl.when(jnp.logical_and(t > 0, has_prev))
            def _():
                move_copy(jnp.maximum(t - 1, 0), c).wait_recv()

            @pl.when(jnp.logical_and(t > 0, jnp.logical_not(has_prev)))
            def _():
                inc_copy(jnp.maximum(t, 1), c).wait()

            send_own(t, c)

        @pl.when(t == 0)
        def _():
            for way in (RIGHT, LEFT):

                @pl.when(has[way])
                def _():
                    mix_copy(way, e).start()

        def arrive(k):
            for c in range(chunks):
                for way, j in ((RIGHT, e - k), (LEFT, e + k)):

                    @pl.when(jnp.logical_and(j >= 0, j < n))
                    def _():
                        ag_copy(way, t, j, c).wait_recv()

                        @pl.when(has[way])
                        def _():
                            ag_copy(way, t, j, c).start()

                        if c == 0:

                            @pl.when(t == 0)
                            def _():
                                mix_copy(way, j).wait_recv()

                                @pl.when(has[way])
                                def _():
                                    mix_copy(way, j).start()

        def step(i, _):
            k = jnp.where(t == 0, lax.rem(i + 1, n), i)
            there_left, there_right = e - k >= 0, e + k < n

            @pl.when(k > 0)
            def _():
                arrive(k)

            both = jnp.logical_and(k > 0, jnp.logical_and(there_left, there_right))
            first = jnp.logical_and(t == 0, i == 0)

            @pl.when(both)
            def _():
                partial_of(t, (e - k, e + k), first)

            @pl.when(jnp.logical_and(jnp.logical_not(both), jnp.logical_or(there_left, there_right)))
            def _():
                partial_of(t, (jnp.where(there_left, e - k, e + k),), first)

            return 0

        lax.fori_loop(0, n, step, 0)

        from_right, from_left = 2 * (n - 1 - e), 2 * e
        last = jnp.maximum(from_right, from_left)

        def combine(time, _):
            for c in range(chunks):
                for way, there, k, j in (
                    (LEFT, has_right, time - from_right, e - (time - from_right)),
                    (RIGHT, has_left, time - from_left, e + (time - from_left)),
                ):

                    @pl.when(
                        jnp.logical_and(
                            there, jnp.logical_and(k >= 0, jnp.logical_and(j >= 0, j < n))
                        )
                    )
                    def _():
                        rs_copy(way, t, j, c).wait_recv()
                        total = held[j, c] + rsin[way, t, j, c].astype(jnp.float32)

                        @pl.when(k == 0)
                        def _():
                            held[j, c] = total

                        @pl.when(k > 0)
                        def _():
                            rsout[t, j, c] = total.astype(jnp.bfloat16)
                            rs_copy(way, t, j, c).start()

                @pl.when(time == last)
                def _():
                    layer = (xbuf[t, e, c].astype(jnp.float32) + held[e, c]).astype(jnp.bfloat16)
                    out[t, :, pl.ds(c * cols, cols)] = layer

                    @pl.when(jnp.logical_and(t < ticks - 1, has_next))
                    def _():
                        moved[jnp.minimum(t, ticks - 2), c] = layer
                        move_copy(jnp.minimum(t, ticks - 2), c).start()

            return 0

        lax.fori_loop(0, 3 * (n - 1) + 1, combine, 0)
        return 0

    lax.fori_loop(0, ticks, tick, 0)

    def drain(j, _):
        for way, within in (
            (RIGHT, jnp.logical_and(has_right, j <= e)),
            (LEFT, jnp.logical_and(has_left, j >= e)),
        ):

            @pl.when(within)
            def _():
                mix_copy(way, j).wait_send()
                for t in range(ticks):
                    for c in range(chunks):
                        ag_copy(way, t, j, c).wait_send()

        for way, within in ((RIGHT, j > e), (LEFT, j < e)):

            @pl.when(within)
            def _():
                for t in range(ticks):
                    for c in range(chunks):
                        rs_copy(way, t, j, c).wait_send()

        return 0

    lax.fori_loop(0, n, drain, 0)

    @pl.when(has_next)
    def _():
        for t in range(ticks - 1):
            for c in range(chunks):
                move_copy(t, c).wait_send()


def solution(mesh):
    n = mesh.shape["expert"]
    sections = mesh.shape["section"]

    def shards(acts, incoming, routes, route_weight, norm_gain, w_gate, w_up, w_down):
        ticks, _, tokens, _ = routes.shape
        width, hidden = w_gate.shape[1:]
        chunks = CHUNKS
        cols = width // chunks
        lanes = -(-tokens // 128) * 128
        table = -(-ticks * EXPERTS // 8) * 8
        half = jnp.bfloat16
        anywhere = pl.BlockSpec(memory_space=pl.ANY)
        vmem = pl.BlockSpec(memory_space=pltpu.VMEM)
        dma = pltpu.SemaphoreType.DMA
        result = pl.pallas_call(
            functools.partial(kernel, n, sections),
            out_shape=jax.ShapeDtypeStruct((ticks, tokens, width), half),
            in_specs=[anywhere, anywhere, vmem, vmem, vmem, anywhere, anywhere, anywhere],
            out_specs=vmem,
            scratch_shapes=[
                pltpu.VMEM((width, hidden), half),
                pltpu.VMEM((width, hidden), half),
                pltpu.VMEM((hidden, width), half),
                pltpu.VMEM((ticks, n, chunks, tokens, cols), half),
                pltpu.VMEM((n, table, lanes), jnp.float32),
                pltpu.VMEM((2, ticks, n, chunks, tokens, cols), half),
                pltpu.VMEM((ticks, n, chunks, tokens, cols), half),
                pltpu.VMEM((n, chunks, tokens, cols), jnp.float32),
                pltpu.VMEM((ticks - 1, chunks, tokens, cols), half),
                dma((3, PIECES)),
                dma((chunks,)),
                dma((ticks, chunks)),
                dma((2, ticks, n, chunks)),
                dma((2, ticks, n, chunks)),
                dma((2, n)),
                dma((2, n)),
                dma((2, ticks, n, chunks)),
                dma((2, ticks, n, chunks)),
                dma((ticks - 1, chunks)),
                dma((ticks - 1, chunks)),
            ],
            compiler_params=pltpu.CompilerParams(
                collective_id=0, has_side_effects=True, vmem_limit_bytes=56 << 20
            ),
        )(
            acts[0],
            incoming,
            jnp.swapaxes(routes, 2, 3),
            jnp.swapaxes(route_weight, 2, 3),
            norm_gain,
            w_gate[0],
            w_up[0],
            w_down[0],
        )
        return result[:, None]

    return jax.shard_map(
        shards,
        mesh=mesh,
        in_specs=(
            P("section", "expert", None),
            P(None, "expert", None),
            P(None, "section", "expert", None),
            P(None, "section", "expert", None),
            P("section", None),
            P("section", None, "expert"),
            P("section", None, "expert"),
            P("section", "expert", None),
        ),
        out_specs=P(None, "section", "expert", None),
        check_vma=False,
    )
```
